128 devices in a mesh: dp: 8 (over y, core), ctx: 16 (over z, x).
Axes of the slice: x: 4, y: 4, z: 4, core: 2. Of those that a mesh axis runs over, the one named last changes fastest.
Arguments:
- queries: bfloat16 [8, 12288, 2048], P('dp', 'ctx'), may hold values from -6 to 6
- keys: bfloat16 [8, 12288, 2048], P('dp', 'ctx'), may hold values from -6 to 6
- values: bfloat16 [8, 12288, 2048], P('dp', 'ctx'), may hold values from -6 to 6
- grad_out: bfloat16 [8, 12288, 2048], P('dp', 'ctx'), may hold values from -6 to 6
- node_ids: int32 [8, 12288], P('dp', 'ctx'), may hold values from 0 to 767, never falling along the last dimension, each value on 1 to 64 neighbouring positions
- flags: int32 [8, 12288], P('dp', 'ctx'), may hold values 0 or 1
- gain: float32 [16], replicated, may hold values from 0.1 to 1.9
Outputs:
- grad_queries: bfloat16 [8, 12288, 2048], P('dp', 'ctx')
- grad_keys: bfloat16 [8, 12288, 2048], P('dp', 'ctx')
- grad_values: bfloat16 [8, 12288, 2048], P('dp', 'ctx')
- grad_gain: float32 [16], replicated
The draws below stay inside these ranges and needn't reach their ends.
Inputs may be any that keep to these rules, and one draw needn't show every extreme that they name: `node_ids`: node numbers never fall along the tokens of a repository; a node spans 1 to 64 tokens.
All inputs are finite; a program needn't handle non-finite values. No bound on the sum of `flags` on one device may be relied on, other than what follows from the above.
Results may differ from the reference program's by a relative error of at most 0.0049.
Values sent between devices are 32-bit elements; how exact they have to be, the bound alone decides.
No kernel may reach another device: no remote copies, remote signals or barrier semaphores. Data moves between devices by JAX's collectives and lax.ppermute only.
A program may use at most 128 MiB of HBM per device.

```python
import math
import jax
import jax.numpy as jnp
import numpy as np
from jax import lax

H = 16
HD = 128
BLOCK = 128
REPOS = 8
TOKENS = 12288
FEAT = 2048
N_DP = 8


def with_ends(drawn, stream_key, smallest, largest):
    spot = [jax.random.randint(jax.random.fold_in(stream_key, axis), (), 0, length) for axis, length in enumerate(drawn.shape)]
    widest = drawn.shape.index(max(drawn.shape))
    next_to = spot[:widest] + [(spot[widest] + 1) % drawn.shape[widest]] + spot[widest + 1:]
    return drawn.at[tuple(spot)].set(smallest).at[tuple(next_to)].set(largest)


def block_scale(key, shape, shards, low, high):
    loudness, own = 1.0, jax.random.fold_in(key, 6)
    for axis_at, parts in shards:
        steps = jnp.exp(jax.random.uniform(jax.random.fold_in(own, axis_at), (parts,), jnp.float32, low / len(shards), high / len(shards)))
        loudness = loudness * jnp.repeat(steps, shape[axis_at] // parts).reshape([-1 if axis == axis_at else 1 for axis in range(len(shape))])
    return loudness


def split_up(count, total, reach, lean):
    portions = [(1 << 20) // math.isqrt(grade ** lean) + 1 for grade in range(2, count + 1)]
    rest, counts = total - reach - (count - 1), [1] * (count - 1)
    while rest > 0:
        free = [i for i in range(count - 1) if counts[i] < reach]
        pool, budget = sum([portions[i] for i in free]), rest
        for i in free:
            addition = min(reach - counts[i], max(1, budget * portions[i] // pool), rest)
            counts[i] = counts[i] + addition
            rest = rest - addition
    return np.array([reach] + counts)


def ragged_sizes(own_key, count, total, reach, lean):
    if count == 2:
        one = jax.random.randint(own_key, (), max(1, total - reach), min(reach, total - 1) + 1)
        return jnp.stack([one, total - one])
    sizes = jnp.asarray(split_up(count, total, reach, lean), jnp.int32)
    couples = (count - 1) // 2
    giver, receiver = sizes[1:1 + 2 * couples:2], sizes[2:2 + 2 * couples:2]
    room = jnp.minimum(giver - 1, reach - receiver)
    passed = jax.random.randint(jax.random.fold_in(own_key, 1), (couples,), 0, 1 << 20) % (room + 1)
    sizes = sizes.at[1:1 + 2 * couples:2].set(giver - passed).at[2:2 + 2 * couples:2].set(receiver + passed)
    return sizes[jax.random.permutation(jax.random.fold_in(own_key, 2), count)]


def noise(stream_key, dims, spread, limit, cuts=(), held_as=jnp.bfloat16):
    entries = jax.random.normal(stream_key, dims, jnp.float32) * spread
    if len(cuts) > 0:
        entries = block_scale(stream_key, dims, cuts, -0.22, 0.18) * entries
    return jnp.clip(entries, min=-limit, max=limit).astype(held_as)


def setup_inputs(seed: int = 0) -> dict:
    seeds = jax.random.split(jax.random.key(seed), 8)
    queries = noise(seeds[0], (REPOS, TOKENS, FEAT), 1.0, 6.0, ((0, 8), (1, 16)))
    keys = noise(seeds[1], (REPOS, TOKENS, FEAT), 1.0, 6.0, ((0, 8), (1, 16)))
    values = noise(seeds[2], (REPOS, TOKENS, FEAT), 1.0, 6.0, ((0, 8), (1, 16)))
    grad_out = noise(seeds[3], (REPOS, TOKENS, FEAT), 1.0, 6.0, ((0, 8), (1, 16)))
    node_ids = jax.vmap(lambda own: jnp.searchsorted(jnp.cumsum(ragged_sizes(own, TOKENS // 16, TOKENS, 64, 1)), jnp.arange(TOKENS), side="right"))(jax.random.split(seeds[4], REPOS)).reshape((REPOS, TOKENS)).astype(jnp.int32)
    flags = with_ends((jax.random.randint(seeds[5], (REPOS, TOKENS), 0, 8) < 1).astype(jnp.int32), jax.random.fold_in(seeds[5], 1), 0, 1)
    gain = jnp.clip(1.0 + 0.18 * jax.random.normal(seeds[6], (H,), jnp.float32), 0.1, 1.9)
    return {"queries": queries, "keys": keys, "values": values, "grad_out": grad_out, "node_ids": node_ids, "flags": flags, "gain": gain}


def to_half(array):
    rounded = array.astype(jnp.bfloat16)
    rounded = lax.optimization_barrier(rounded)
    return rounded.astype(jnp.float32)

def one_repo(items):
    queries, keys, values, grad_out, node_ids, flags, gain = items
    count = TOKENS // BLOCK
    scale = 1.0 / math.sqrt(HD * TOKENS)
    q_blk = queries.reshape(count, BLOCK, H, HD).astype(jnp.float32)
    k_blk = keys.reshape(count, BLOCK, H, HD).astype(jnp.float32)
    v_blk = values.reshape(count, BLOCK, H, HD).astype(jnp.float32)
    g_blk = grad_out.reshape(count, BLOCK, H, HD).astype(jnp.float32)
    nodes = node_ids.reshape(count, BLOCK)
    marks = flags.reshape(count, BLOCK)
    rows = lax.broadcasted_iota(jnp.int32, (BLOCK, BLOCK), 0)
    cols = lax.broadcasted_iota(jnp.int32, (BLOCK, BLOCK), 1)
    causal = (cols <= rows)[None]
    linked = (nodes[:, :, None] == nodes[:, None, :]) | (marks[:, None, :] == 1)
    seen = (causal & linked).astype(jnp.float32)[:, None]
    scores = jnp.einsum('bthd,bshd->bhts', q_blk, k_blk) * seen
    dscores = jnp.einsum('bthd,bshd->bhts', g_blk, v_blk) * seen
    intra_term = lax.optimization_barrier(jnp.sum(scores * dscores, axis=(0, 2, 3)))
    pm = to_half(scores)
    dpm = to_half(dscores)
    kv_blk = jnp.einsum('bshd,bshe->bhde', k_blk, v_blk)
    qg_blk = jnp.einsum('bthd,bthe->bhde', q_blk, g_blk)
    zero = jnp.zeros((1,) + kv_blk.shape[1:], jnp.float32)
    prior = jnp.cumsum(jnp.concatenate([zero, kv_blk[:-1]], axis=0), axis=0)
    later = jnp.flip(jnp.cumsum(jnp.flip(jnp.concatenate([qg_blk[1:], zero], axis=0), 0), axis=0), 0)
    inter_term = lax.optimization_barrier(jnp.sum(prior * qg_blk, axis=(0, 2, 3)))
    prior_h = to_half(prior)
    later_h = to_half(later)
    factor = (scale * gain)[None, None, :, None]
    dq = jnp.einsum('bhts,bshd->bthd', dpm, k_blk) + jnp.einsum('bthe,bhde->bthd', g_blk, prior_h)
    dk = jnp.einsum('bhts,bthd->bshd', dpm, q_blk) + jnp.einsum('bshe,bhde->bshd', v_blk, later_h)
    dv = jnp.einsum('bhts,bthd->bshd', pm, g_blk) + jnp.einsum('bshd,bhde->bshe', k_blk, later_h)
    shape = (TOKENS, H * HD)
    return ((dq * factor).astype(jnp.bfloat16).reshape(shape), (dk * factor).astype(jnp.bfloat16).reshape(shape), (dv * factor).astype(jnp.bfloat16).reshape(shape), scale * (intra_term + inter_term))

def reference(queries, keys, values, grad_out, node_ids, flags, gain):
    repos = queries.shape[0]
    gains = jnp.broadcast_to(gain, (repos,) + gain.shape)
    dq, dk, dv, terms = lax.map(one_repo, (queries, keys, values, grad_out, node_ids, flags, gains))
    grad_gain = lax.optimization_barrier(jnp.sum(terms, axis=0)) / math.sqrt(N_DP * TOKENS * HD)
    return (dq, dk, dv, grad_gain.astype(jnp.float32))
```

```python
import functools
import math

import jax
import jax.numpy as jnp
from jax import lax
from jax.experimental import pallas as pl
from jax.experimental.pallas import tpu as pltpu
from jax.sharding import PartitionSpec as P

H = 16
HD = 128
BLOCK = 128
ROW = 4
COL = 4
GROUP = H // ROW
WIDE = GROUP * HD


def dot(a, b, dims):
    return lax.dot_general(a, b, (dims, ((), ())), preferred_element_type=jnp.float32)


def over_rows(a, b):
    return dot(a, b, ((0,), (0,)))


def over_cols(a, b):
    return dot(a, b, ((1,), (1,)))


def plain(a, b):
    return dot(a, b, ((1,), (0,)))


def head(ref, j, rows=slice(None)):
    return ref[rows, j * HD:(j + 1) * HD]


def params(vmem):
    return pltpu.CompilerParams(dimension_semantics=("arbitrary",), vmem_limit_bytes=vmem)


def state_kernel(spot, a_ref, b_ref, *outs):
    step = pl.program_id(0)
    for at, out in enumerate(outs):
        @pl.when(step == at)
        def _():
            for j in range(GROUP):
                out[j] = over_rows(head(a_ref, j), head(b_ref, j))


def own_states(spot, a, b):
    length = a.shape[1]
    wide = pl.BlockSpec((None, length, WIDE), lambda o, s: (0, 0, (s[0] + o) % ROW))
    return pl.pallas_call(
        state_kernel,
        grid_spec=pltpu.PrefetchScalarGridSpec(
            num_scalar_prefetch=1,
            grid=(ROW,),
            in_specs=[wide, wide],
            out_specs=[pl.BlockSpec((GROUP, HD, HD), lambda o, s: (0, 0, 0))] * ROW,
        ),
        out_shape=[jax.ShapeDtypeStruct((GROUP, HD, HD), jnp.float32)] * ROW,
        compiler_params=params(16 << 20),
        cost_estimate=pl.CostEstimate(
            flops=2 * length * H * HD * HD, bytes_accessed=4 * length * H * HD, transcendentals=0
        ),
        name="own_states",
    )(spot, a, b)


NEAR_HEADS = 2


def near_kernel(count, q_ref, k_ref, v_ref, g_ref, nodes_ref, marks_ref, pm_ref, dpm_ref, term_ref, seen_ref):
    @pl.when(pl.program_id(0) == 0)
    def _():
        rows = lax.broadcasted_iota(jnp.int32, (BLOCK, BLOCK), 0)
        cols = lax.broadcasted_iota(jnp.int32, (BLOCK, BLOCK), 1)
        for b in range(count):
            part = slice(b * BLOCK, (b + 1) * BLOCK)
            across = jnp.broadcast_to(nodes_ref[0:1, part], (BLOCK, BLOCK))
            down = across.T
            marks = jnp.broadcast_to(marks_ref[0:1, part], (BLOCK, BLOCK))
            seen = (cols <= rows) & ((across == down) | (marks == 1))
            seen_ref[b] = seen.astype(jnp.float32)

    for j in range(NEAR_HEADS):
        term = jnp.zeros((BLOCK, BLOCK), jnp.float32)
        prior = None
        for b in range(count):
            part = slice(b * BLOCK, (b + 1) * BLOCK)
            q, k, v, g = (head(ref, j, part) for ref in (q_ref, k_ref, v_ref, g_ref))
            seen = seen_ref[b]
            scores = over_cols(q, k) * seen
            dscores = over_cols(g, v) * seen
            term = term + scores * dscores
            pm_ref[j, part] = scores.astype(jnp.bfloat16)
            dpm_ref[j, part] = dscores.astype(jnp.bfloat16)
            if prior is not None:
                term = term + prior * over_rows(q, g)
            if b < count - 1:
                kv = over_rows(k, v)
                prior = kv if prior is None else prior + kv
        term_ref[j] = jnp.sum(term.reshape(BLOCK // 8, 8, BLOCK), axis=0)


def near(q, k, v, g, nodes, marks):
    length = q.shape[1]
    count = length // BLOCK
    wide = pl.BlockSpec((None, length, NEAR_HEADS * HD), lambda i: (0, 0, i))
    flat = pl.BlockSpec((1, length), lambda i: (0, 0))
    scores = pl.BlockSpec((NEAR_HEADS, length, BLOCK), lambda i: (i, 0, 0))
    return pl.pallas_call(
        functools.partial(near_kernel, count),
        grid=(H // NEAR_HEADS,),
        in_specs=[wide] * 4 + [flat] * 2,
        out_specs=[scores, scores, pl.BlockSpec((NEAR_HEADS, 8, BLOCK), lambda i: (i, 0, 0))],
        out_shape=[
            jax.ShapeDtypeStruct((H, length, BLOCK), jnp.bfloat16),
            jax.ShapeDtypeStruct((H, length, BLOCK), jnp.bfloat16),
            jax.ShapeDtypeStruct((H, 8, BLOCK), jnp.float32),
        ],
        scratch_shapes=[pltpu.VMEM((count, BLOCK, BLOCK), jnp.float32)],
        compiler_params=params(16 << 20),
        cost_estimate=pl.CostEstimate(
            flops=8 * length * H * HD * HD, bytes_accessed=12 * length * H * HD, transcendentals=0
        ),
        name="near",
    )(q, k, v, g, nodes, marks)


def pick(step, states, held):
    for at, ref in enumerate(states):
        @pl.when(step == at)
        def _():
            held[...] = ref[...]


def factor_of(spot, gain_ref, scale, j):
    group = (spot[0] + ROW - pl.program_id(0)) % ROW
    return gain_ref[group * GROUP + j] * scale


def dq_kernel(count, scale, spot, k_ref, v_ref, g_ref, dpm_ref, gain_ref, s0, s1, s2, s3, dq_ref, held):
    pick(pl.program_id(0), (s0, s1, s2, s3), held)
    for j in range(GROUP):
        factor = factor_of(spot, gain_ref, scale, j)
        prior = held[j]
        for b in range(count):
            part = slice(b * BLOCK, (b + 1) * BLOCK)
            k, v, g = (head(ref, j, part) for ref in (k_ref, v_ref, g_ref))
            dq = plain(dpm_ref[j, part], k) + over_cols(g, prior.astype(jnp.bfloat16))
            dq_ref[part, j * HD:(j + 1) * HD] = (dq * factor).astype(jnp.bfloat16)
            if b < count - 1:
                prior = prior + over_rows(k, v)


def dkv_kernel(count, scale, spot, q_ref, k_ref, v_ref, g_ref, pm_ref, dpm_ref, gain_ref, s0, s1, s2, s3,
               dk_ref, dv_ref, held):
    pick(pl.program_id(0), (s0, s1, s2, s3), held)
    for j in range(GROUP):
        factor = factor_of(spot, gain_ref, scale, j)
        later = held[j]
        for b in reversed(range(count)):
            part = slice(b * BLOCK, (b + 1) * BLOCK)
            q, k, v, g = (head(ref, j, part) for ref in (q_ref, k_ref, v_ref, g_ref))
            late = later.astype(jnp.bfloat16)
            dk = over_rows(dpm_ref[j, part], q) + over_cols(v, late)
            dv = over_rows(pm_ref[j, part], g) + plain(k, late)
            dk_ref[part, j * HD:(j + 1) * HD] = (dk * factor).astype(jnp.bfloat16)
            dv_ref[part, j * HD:(j + 1) * HD] = (dv * factor).astype(jnp.bfloat16)
            if b > 0:
                later = later + over_rows(q, g)


def far(kernel, scale, spot, wides, scores, gain, states, outputs, name):
    length = wides[0].shape[1]
    count = length // BLOCK

    def group(o, s):
        return (s[0] + ROW - o) % ROW

    wide = pl.BlockSpec((None, length, WIDE), lambda o, s: (0, 0, group(o, s)))
    score = pl.BlockSpec((GROUP, length, BLOCK), lambda o, s: (group(o, s), 0, 0))
    whole = pl.BlockSpec((GROUP, HD, HD), lambda o, s: (0, 0, 0))
    return pl.pallas_call(
        functools.partial(kernel, count, scale),
        grid_spec=pltpu.PrefetchScalarGridSpec(
            num_scalar_prefetch=1,
            grid=(ROW,),
            in_specs=[wide] * len(wides) + [score] * len(scores) + [pl.BlockSpec(memory_space=pltpu.SMEM)]
            + [whole] * ROW,
            out_specs=[wide] * outputs,
            scratch_shapes=[pltpu.VMEM((GROUP, HD, HD), jnp.float32)],
        ),
        out_shape=[jax.ShapeDtypeStruct(wides[0].shape, jnp.bfloat16)] * outputs,
        compiler_params=params(24 << 20),
        cost_estimate=pl.CostEstimate(
            flops=2 * (2 * outputs + 1) * length * H * HD * HD,
            bytes_accessed=2 * (len(wides) + len(scores) + outputs) * length * H * HD,
            transcendentals=0,
        ),
        name=name,
    )(spot, *wides, *scores, gain, *states)


def along_row(block, distance):
    route = [(z * ROW + x, z * ROW + (x + distance) % ROW) for z in range(COL) for x in range(ROW)]
    return lax.ppermute(block, "ctx", route)


def along_column(block, distance, around=False):
    route = [
        (z * ROW + x, (z + distance) % COL * ROW + x)
        for z in range(COL) for x in range(ROW)
        if around or 0 <= z + distance < COL
    ]
    return lax.ppermute(block, "ctx", route)


def to_owners(own):
    return [own[0]] + [along_row(own[o], o) for o in range(1, ROW)]


def other_rows(parts, sign):
    total = (parts[0] + parts[1]) + (parts[2] + parts[3])
    got = [along_column(total, sign * o) for o in range(1, COL)]
    return got[0] + got[1] + got[2]


def scanned(parts, base, spot, before):
    outs = []
    for p in range(ROW):
        target = (spot + p) % ROW
        acc = base
        for o in range(ROW):
            source = (spot + ROW - o) % ROW
            counts = source < target if before else source > target
            acc = acc + jnp.where(counts, parts[o], 0.0)
        outs.append(acc)
    return outs


def everywhere(term):
    def added(value, moves):
        return (value + moves(2)) + (moves(1) + moves(3))

    term = added(term, lambda o: along_row(term, o))
    term_x = term
    term = added(term_x, lambda o: along_column(term_x, o, True))
    term_z = term
    cores = lax.axis_size("dp") // 4

    def along_y(o):
        route = [(y * cores + n, (y + o) % 4 * cores + n) for y in range(4) for n in range(cores)]
        return lax.ppermute(term_z, "dp", route)

    term = added(term_z, along_y)
    return term + lax.ppermute(term, "dp", [(i, i ^ 1) for i in range(lax.axis_size("dp"))])


def on_device(queries, keys, values, grad_out, node_ids, flags, gain):
    length = queries.shape[1]
    scale = 1.0 / math.sqrt(HD * length * lax.axis_size("ctx"))
    spot = lax.axis_index("ctx") % ROW
    spots = spot.astype(jnp.int32)[None]

    kv_own = own_states(spots, keys, values)
    kv_parts = to_owners(kv_own)
    qg_own = own_states(spots, queries, grad_out)
    qg_parts = to_owners(qg_own)
    pm, dpm, own_term = near(queries, keys, values, grad_out, node_ids, flags)

    kv_base = other_rows(kv_parts, 1)
    kv_out = scanned(kv_parts, kv_base, spot, True)
    kv_back = [kv_out[0]] + [along_row(kv_out[p], p) for p in range(1, ROW)]
    qg_base = other_rows(qg_parts, -1)
    qg_out = scanned(qg_parts, qg_base, spot, False)
    qg_back = [qg_out[0]] + [along_row(qg_out[p], p) for p in range(1, ROW)]

    cross = sum(jnp.sum(kv_out[p] * qg_parts[(ROW - p) % ROW], axis=(1, 2)) for p in range(ROW))
    mine = lax.broadcasted_iota(jnp.int32, (ROW, GROUP), 0) == spot
    term = jnp.sum(own_term, axis=(1, 2)) + jnp.where(mine, cross[None], 0.0).reshape(H)
    total = everywhere(scale * term)
    norm_tokens = lax.axis_size("dp") * length * lax.axis_size("ctx") * HD
    grad_gain = total / math.sqrt(norm_tokens)

    (grad_queries,) = far(
        dq_kernel, scale, spots, (keys, values, grad_out), (dpm,), gain, kv_back, 1, "grad_q"
    )
    grad_keys, grad_values = far(
        dkv_kernel, scale, spots, (queries, keys, values, grad_out), (pm, dpm), gain, qg_back, 2, "grad_kv"
    )
    return (grad_queries, grad_keys, grad_values, grad_gain)


def solution(mesh):
    placed = (
        P("dp", "ctx", None),
        P("dp", "ctx", None),
        P("dp", "ctx", None),
        P("dp", "ctx", None),
        P("dp", "ctx"),
        P("dp", "ctx"),
        P(),
    )
    return jax.shard_map(
        on_device,
        mesh=mesh,
        in_specs=placed,
        out_specs=(P("dp", "ctx", None), P("dp", "ctx", None), P("dp", "ctx", None), P()),
        check_vma=False,
    )
```

```python
import functools
import math

import jax
import jax.numpy as jnp
from jax import lax
from jax.experimental import pallas as pl
from jax.experimental.pallas import tpu as pltpu
from jax.sharding import PartitionSpec as P

H = 16
HD = 128
BLOCK = 128
TILE = 8


def dot(a, b, dims):
    return lax.dot_general(a, b, (dims, ((), ())), preferred_element_type=jnp.float32)


def over_rows(a, b):
    return dot(a, b, ((0,), (0,)))


def over_cols(a, b):
    return dot(a, b, ((1,), (1,)))


def plain(a, b):
    return dot(a, b, ((1,), (0,)))


def head(ref, j, rows=slice(None)):
    return ref[rows, j * HD:(j + 1) * HD]


def parted(state):
    high = state.astype(jnp.bfloat16)
    return high, (state - high.astype(jnp.float32)).astype(jnp.bfloat16)


def times_transposed(rows, parts):
    return over_cols(jnp.concatenate([rows, rows], axis=1), jnp.concatenate(parts, axis=1))


def times(rows, parts):
    return plain(jnp.concatenate([rows, rows], axis=1), jnp.concatenate(parts, axis=0))


def cost(flops, bytes_accessed):
    return pl.CostEstimate(flops=flops, bytes_accessed=bytes_accessed, transcendentals=0)


FULL = 60 * 1024 * 1024


def params(vmem):
    return pltpu.CompilerParams(vmem_limit_bytes=vmem)


CHUNKS = 8


def state_kernel(*refs):
    sources, out_ref, kept, sems = refs[:4], refs[4], refs[5:9], refs[9]
    wide = sources[0].shape[2] // CHUNKS
    heads = wide // HD

    def copy(i, n):
        columns = slice(n * wide, (n + 1) * wide)
        return pltpu.make_async_copy(
            sources[i].at[0, :, columns], kept[i].at[:, columns], sems.at[i, n]
        )

    for n in range(CHUNKS):
        for i in range(4):
            copy(i, n).start()
    for n in range(CHUNKS):
        for i in range(4):
            copy(i, n).wait()
        for j in range(n * heads, (n + 1) * heads):
            q, k, v, g = (head(ref, j) for ref in kept)
            out_ref[j, 0:HD] = over_rows(k, v)
            out_ref[j, HD:2 * HD] = over_rows(q, g)


def own_states(q, k, v, g):
    _, length, features = q.shape
    return pl.pallas_call(
        state_kernel,
        in_specs=[pl.BlockSpec(memory_space=pltpu.HBM)] * 4,
        out_specs=pl.BlockSpec(memory_space=pltpu.VMEM),
        out_shape=jax.ShapeDtypeStruct((H, 2 * HD, HD), jnp.float32),
        scratch_shapes=[pltpu.VMEM((length, features), jnp.bfloat16)] * 4
        + [pltpu.SemaphoreType.DMA((4, CHUNKS))],
        compiler_params=params(FULL),
        cost_estimate=cost(4 * length * H * HD * HD, 8 * length * H * HD),
        name="own_states",
    )(q, k, v, g)


NEAR_HEADS = 1


def rows_of(b):
    return slice(b * BLOCK, (b + 1) * BLOCK)


def visible(nodes_ref, marks_ref, b):
    rows = lax.broadcasted_iota(jnp.int32, (BLOCK, BLOCK), 0)
    cols = lax.broadcasted_iota(jnp.int32, (BLOCK, BLOCK), 1)
    across = jnp.broadcast_to(nodes_ref[0:1, rows_of(b)], (BLOCK, BLOCK))
    marks = jnp.broadcast_to(marks_ref[0:1, rows_of(b)], (BLOCK, BLOCK))
    return ((cols <= rows) & ((across == across.T) | (marks == 1))).astype(jnp.float32)


def near_q_kernel(count, q_ref, k_ref, v_ref, g_ref, nodes_ref, marks_ref, dq_ref, term_ref, seen_ref):
    @pl.when(pl.program_id(0) == 0)
    def _():
        for b in range(count):
            seen_ref[b] = visible(nodes_ref, marks_ref, b)

    for j in range(NEAR_HEADS):
        term = jnp.zeros((BLOCK, BLOCK), jnp.float32)
        earlier = None
        for b in range(count):
            q, k, v, g = (head(ref, j, rows_of(b)) for ref in (q_ref, k_ref, v_ref, g_ref))
            seen = seen_ref[b]
            dscores = over_cols(g, v) * seen
            term = term + over_cols(q, k) * dscores
            dq = plain(dscores.astype(jnp.bfloat16), k)
            if earlier is not None:
                term = term + earlier * over_rows(q, g)
                dq = dq + times_transposed(g, parted(earlier))
            dq_ref[rows_of(b), j * HD:(j + 1) * HD] = dq
            if b < count - 1:
                kv = over_rows(k, v)
                earlier = kv if earlier is None else earlier + kv
        term_ref[j] = jnp.sum(term.reshape(BLOCK // 8, 8, BLOCK), axis=0)


def near_kv_kernel(count, q_ref, k_ref, v_ref, g_ref, nodes_ref, marks_ref, dk_ref, dv_ref, seen_ref):
    @pl.when(pl.program_id(0) == 0)
    def _():
        for b in range(count):
            seen_ref[b] = visible(nodes_ref, marks_ref, b).T

    for j in range(NEAR_HEADS):
        later = None
        for b in reversed(range(count)):
            q, k, v, g = (head(ref, j, rows_of(b)) for ref in (q_ref, k_ref, v_ref, g_ref))
            seen = seen_ref[b]
            dk = plain((over_cols(v, g) * seen).astype(jnp.bfloat16), q)
            dv = plain((over_cols(k, q) * seen).astype(jnp.bfloat16), g)
            if later is not None:
                parts = parted(later)
                dk = dk + times_transposed(v, parts)
                dv = dv + times(k, parts)
            dk_ref[rows_of(b), j * HD:(j + 1) * HD] = dk
            dv_ref[rows_of(b), j * HD:(j + 1) * HD] = dv
            if b > 0:
                qg = over_rows(q, g)
                later = qg if later is None else later + qg


def near(kernel, inputs, nodes, marks, outputs, terms, name):
    _, length, features = inputs[0].shape
    count = length // BLOCK
    wide = pl.BlockSpec((None, length, NEAR_HEADS * HD), lambda i: (0, 0, i))
    flat = pl.BlockSpec((1, length), lambda i: (0, 0))
    term = pl.BlockSpec((NEAR_HEADS, 8, BLOCK), lambda i: (i, 0, 0))
    return pl.pallas_call(
        functools.partial(kernel, count),
        grid=(H // NEAR_HEADS,),
        in_specs=[wide] * 4 + [flat] * 2,
        out_specs=[wide] * outputs + [term] * terms,
        out_shape=[jax.ShapeDtypeStruct((1, length, features), jnp.float32)] * outputs
        + [jax.ShapeDtypeStruct((H, 8, BLOCK), jnp.float32)] * terms,
        scratch_shapes=[pltpu.VMEM((count, BLOCK, BLOCK), jnp.float32)],
        compiler_params=params(FULL),
        cost_estimate=cost(28 * length * H * HD * HD, 20 * length * H * HD),
        name=name,
    )(*inputs, nodes, marks)


def scan_kernel(spot_ref, own_ref, local_ref, out_ref):
    devices = own_ref.shape[0]
    total = jnp.zeros((HD, HD), jnp.float32)
    cross = jnp.zeros((HD, HD), jnp.float32)
    for at in range(devices):
        out_ref[at, 0:HD] = total
        cross = cross + total * own_ref[at, HD:2 * HD]
        total = total + own_ref[at, 0:HD]
    total = jnp.zeros((HD, HD), jnp.float32)
    for at in reversed(range(devices)):
        out_ref[at, HD:2 * HD] = total
        total = total + own_ref[at, HD:2 * HD]
    cross = jnp.sum(jnp.sum(cross, axis=0, keepdims=True), axis=1, keepdims=True)
    lanes = lax.broadcasted_iota(jnp.int32, (TILE, HD), 1)
    terms = local_ref[...] + jnp.where(lanes == spot_ref[0], cross, 0.0)
    for at in range(devices):
        out_ref[at, 2 * HD:2 * HD + TILE] = terms


def scan(spot, own, local):
    whole = pl.BlockSpec(memory_space=pltpu.VMEM)
    return pl.pallas_call(
        scan_kernel,
        in_specs=[pl.BlockSpec(memory_space=pltpu.SMEM), whole, whole],
        out_specs=whole,
        out_shape=jax.ShapeDtypeStruct((own.shape[0], 2 * HD + TILE, HD), jnp.float32),
        compiler_params=params(FULL),
        cost_estimate=cost(3 * own.size, 8 * own.size),
        name="scan",
    )(spot, own, local)


FAR_HEADS = 2


def far_kernel(scale, gain_ref, k_ref, v_ref, g_ref, part_q_ref, part_k_ref, part_v_ref, state_ref,
               dq_ref, dk_ref, dv_ref):
    for j in range(FAR_HEADS):
        columns = slice(j * HD, (j + 1) * HD)
        factor = gain_ref[pl.program_id(0) * FAR_HEADS + j] * scale
        prior = parted(state_ref[j, 0:HD])
        later = parted(state_ref[j, HD:2 * HD])
        dq = part_q_ref[:, columns] + times_transposed(g_ref[:, columns], prior)
        dq_ref[:, columns] = (dq * factor).astype(jnp.bfloat16)
        dk = part_k_ref[:, columns] + times_transposed(v_ref[:, columns], later)
        dk_ref[:, columns] = (dk * factor).astype(jnp.bfloat16)
        dv = part_v_ref[:, columns] + times(k_ref[:, columns], later)
        dv_ref[:, columns] = (dv * factor).astype(jnp.bfloat16)


def far(scale, gain, k, v, g, parts, states):
    _, length, features = k.shape
    wide = pl.BlockSpec((None, length, FAR_HEADS * HD), lambda i: (0, 0, i))
    state = pl.BlockSpec((FAR_HEADS, 2 * HD, HD), lambda i: (i, 0, 0))
    return pl.pallas_call(
        functools.partial(far_kernel, scale),
        grid=(H // FAR_HEADS,),
        in_specs=[pl.BlockSpec(memory_space=pltpu.SMEM)] + [wide] * 6 + [state],
        out_specs=[wide] * 3,
        out_shape=[jax.ShapeDtypeStruct((1, length, features), jnp.bfloat16)] * 3,
        compiler_params=params(FULL),
        cost_estimate=cost(12 * length * H * HD * HD, 24 * length * H * HD),
        name="far",
    )(gain, k, v, g, *parts, states)


def exchange(block, axis):
    return lax.all_to_all(block, axis, 0, 0, tiled=True)


def on_device(queries, keys, values, grad_out, node_ids, flags, gain):
    length = queries.shape[1]
    scale = 1.0 / math.sqrt(HD * length * lax.axis_size("ctx"))
    spot = lax.axis_index("ctx").astype(jnp.int32)[None]

    inputs = (queries, keys, values, grad_out)
    owned = exchange(own_states(*inputs), "ctx")
    part_q, own_term = near(near_q_kernel, inputs, node_ids, flags, 1, 1, "near_q")
    part_k, part_v = near(near_kv_kernel, inputs, node_ids, flags, 2, 0, "near_kv")
    local = jnp.pad(jnp.sum(own_term, axis=(1, 2)), (0, HD - H))[None]
    states = exchange(scan(spot, owned, jnp.broadcast_to(local, (TILE, HD))), "ctx")

    terms = jnp.sum(states[:, 2 * HD:, :], axis=0)
    terms = exchange(jnp.broadcast_to(terms, (lax.axis_size("dp"), TILE, HD)), "dp")
    norm_tokens = lax.axis_size("dp") * length * lax.axis_size("ctx") * HD
    grad_gain = jnp.sum(terms, axis=0)[0, :H] * scale / math.sqrt(norm_tokens)

    return (*far(scale, gain, keys, values, grad_out, (part_q, part_k, part_v), states), grad_gain)


def solution(mesh):
    placed = (
        P("dp", "ctx", None),
        P("dp", "ctx", None),
        P("dp", "ctx", None),
        P("dp", "ctx", None),
        P("dp", "ctx"),
        P("dp", "ctx"),
        P(),
    )
    return jax.shard_map(
        on_device,
        mesh=mesh,
        in_specs=placed,
        out_specs=(P("dp", "ctx", None), P("dp", "ctx", None), P("dp", "ctx", None), P()),
        check_vma=False,
    )
```

```python
import functools
import math

import jax
import jax.numpy as jnp
from jax import lax
from jax.experimental import pallas as pl
from jax.experimental.pallas import tpu as pltpu
from jax.sharding import PartitionSpec as P

H = 16
HD = 128
BLOCK = 128
TILE = 8


def dot(a, b, dims):
    return lax.dot_general(a, b, (dims, ((), ())), preferred_element_type=jnp.float32)


def over_rows(a, b):
    return dot(a, b, ((0,), (0,)))


def over_cols(a, b):
    return dot(a, b, ((1,), (1,)))


def plain(a, b):
    return dot(a, b, ((1,), (0,)))


def head(ref, j, rows=slice(None)):
    return ref[rows, j * HD:(j + 1) * HD]


def parted(state):
    high = state.astype(jnp.bfloat16)
    return high, (state - high.astype(jnp.float32)).astype(jnp.bfloat16)


def times_transposed(rows, parts):
    return over_cols(jnp.concatenate([rows, rows], axis=1), jnp.concatenate(parts, axis=1))


def times(rows, parts):
    return plain(jnp.concatenate([rows, rows], axis=1), jnp.concatenate(parts, axis=0))


def cost(flops, bytes_accessed):
    return pl.CostEstimate(flops=flops, bytes_accessed=bytes_accessed, transcendentals=0)


FULL = 60 * 1024 * 1024


def params(vmem):
    return pltpu.CompilerParams(vmem_limit_bytes=vmem)


CHUNKS = 4


def state_kernel(*refs):
    sources, out_ref, kept, sems = refs[:4], refs[4], refs[5:9], refs[9]
    wide = sources[0].shape[2] // CHUNKS
    heads = wide // HD

    def copy(i, n):
        columns = slice(n * wide, (n + 1) * wide)
        return pltpu.make_async_copy(
            sources[i].at[0, :, columns], kept[i].at[:, columns], sems.at[i, n]
        )

    for n in range(CHUNKS):
        for i in range(4):
            copy(i, n).start()
    for n in range(CHUNKS):
        for i in range(4):
            copy(i, n).wait()
        for j in range(n * heads, (n + 1) * heads):
            q, k, v, g = (head(ref, j) for ref in kept)
            out_ref[j, 0:HD] = over_rows(k, v)
            out_ref[j, HD:2 * HD] = over_rows(q, g)


def own_states(q, k, v, g):
    _, length, features = q.shape
    return pl.pallas_call(
        state_kernel,
        in_specs=[pl.BlockSpec(memory_space=pltpu.HBM)] * 4,
        out_specs=pl.BlockSpec(memory_space=pltpu.VMEM),
        out_shape=jax.ShapeDtypeStruct((H, 2 * HD, HD), jnp.float32),
        scratch_shapes=[pltpu.VMEM((length, features), jnp.bfloat16)] * 4
        + [pltpu.SemaphoreType.DMA((4, CHUNKS))],
        compiler_params=params(FULL),
        cost_estimate=cost(4 * length * H * HD * HD, 8 * length * H * HD),
        name="own_states",
    )(q, k, v, g)


NEAR_HEADS = 2


def summed(block):
    return jnp.sum(jnp.sum(block, axis=0, keepdims=True), axis=1, keepdims=True)


def rows_of(b):
    return slice(b * BLOCK, (b + 1) * BLOCK)


def visible(nodes_ref, marks_ref, b):
    rows = lax.broadcasted_iota(jnp.int32, (BLOCK, BLOCK), 0)
    cols = lax.broadcasted_iota(jnp.int32, (BLOCK, BLOCK), 1)
    across = jnp.broadcast_to(nodes_ref[0:1, rows_of(b)], (BLOCK, BLOCK))
    marks = jnp.broadcast_to(marks_ref[0:1, rows_of(b)], (BLOCK, BLOCK))
    return ((cols <= rows) & ((across == across.T) | (marks == 1))).astype(jnp.float32)


def near_q_kernel(count, q_ref, k_ref, v_ref, g_ref, nodes_ref, marks_ref, dq_ref, term_ref, seen_ref):
    @pl.when(pl.program_id(0) == 0)
    def _():
        for b in range(count):
            seen_ref[b] = visible(nodes_ref, marks_ref, b)
        term_ref[...] = jnp.zeros_like(term_ref)

    for j in range(NEAR_HEADS):
        term = jnp.zeros((BLOCK, BLOCK), jnp.float32)
        earlier = None
        for b in range(count):
            q, k, v, g = (head(ref, j, rows_of(b)) for ref in (q_ref, k_ref, v_ref, g_ref))
            seen = seen_ref[b]
            dscores = over_cols(g, v) * seen
            term = term + over_cols(q, k) * dscores
            dq = plain(dscores.astype(jnp.bfloat16), k)
            if earlier is not None:
                term = term + earlier * over_rows(q, g)
                dq = dq + times_transposed(g, parted(earlier))
            dq_ref[rows_of(b), j * HD:(j + 1) * HD] = dq.astype(jnp.bfloat16)
            if b < count - 1:
                kv = over_rows(k, v)
                earlier = kv if earlier is None else earlier + kv
        lanes = lax.broadcasted_iota(jnp.int32, (TILE, HD), 1)
        here = lanes == pl.program_id(0) * NEAR_HEADS + j
        term_ref[...] += jnp.where(here, summed(term), 0.0)


def near_kv_kernel(count, q_ref, k_ref, v_ref, g_ref, nodes_ref, marks_ref, dk_ref, dv_ref, seen_ref):
    @pl.when(pl.program_id(0) == 0)
    def _():
        for b in range(count):
            seen_ref[b] = visible(nodes_ref, marks_ref, b).T

    for j in range(NEAR_HEADS):
        later = None
        for b in reversed(range(count)):
            q, k, v, g = (head(ref, j, rows_of(b)) for ref in (q_ref, k_ref, v_ref, g_ref))
            seen = seen_ref[b]
            dk = plain((over_cols(v, g) * seen).astype(jnp.bfloat16), q)
            dv = plain((over_cols(k, q) * seen).astype(jnp.bfloat16), g)
            if later is not None:
                parts = parted(later)
                dk = dk + times_transposed(v, parts)
                dv = dv + times(k, parts)
            dk_ref[rows_of(b), j * HD:(j + 1) * HD] = dk.astype(jnp.bfloat16)
            dv_ref[rows_of(b), j * HD:(j + 1) * HD] = dv.astype(jnp.bfloat16)
            if b > 0:
                qg = over_rows(q, g)
                later = qg if later is None else later + qg


def near(kernel, inputs, nodes, marks, outputs, terms, name):
    _, length, features = inputs[0].shape
    count = length // BLOCK
    wide = pl.BlockSpec((None, length, NEAR_HEADS * HD), lambda i: (0, 0, i))
    flat = pl.BlockSpec((1, length), lambda i: (0, 0))
    term = pl.BlockSpec((TILE, HD), lambda i: (0, 0))
    return pl.pallas_call(
        functools.partial(kernel, count),
        grid=(H // NEAR_HEADS,),
        in_specs=[wide] * 4 + [flat] * 2,
        out_specs=[wide] * outputs + [term] * terms,
        out_shape=[jax.ShapeDtypeStruct((1, length, features), jnp.bfloat16)] * outputs
        + [jax.ShapeDtypeStruct((TILE, HD), jnp.float32)] * terms,
        scratch_shapes=[pltpu.VMEM((count, BLOCK, BLOCK), jnp.float32)],
        compiler_params=params(FULL),
        cost_estimate=cost(28 * length * H * HD * HD, 20 * length * H * HD),
        name=name,
    )(*inputs, nodes, marks)


def scan_kernel(spot_ref, own_ref, local_ref, out_ref, held, gained, sems, sem):
    devices = own_ref.shape[0]
    local = pltpu.make_async_copy(local_ref, gained, sem)
    local.start()

    def copy(at, late):
        rows = slice(HD, 2 * HD + TILE) if late else slice(0, HD)
        return pltpu.make_async_copy(held.at[at, rows], out_ref.at[at, rows], sems.at[at, late])

    total = jnp.zeros((HD, HD), jnp.float32)
    cross = jnp.zeros((HD, HD), jnp.float32)
    for at in range(devices):
        held[at, 0:HD] = total
        copy(at, 0).start()
        cross = cross + total * own_ref[at, HD:2 * HD]
        total = total + own_ref[at, 0:HD]
    lanes = lax.broadcasted_iota(jnp.int32, (TILE, HD), 1)
    local.wait()
    terms = gained[...] + jnp.where(lanes == spot_ref[0], summed(cross), 0.0)
    total = jnp.zeros((HD, HD), jnp.float32)
    for at in reversed(range(devices)):
        held[at, HD:2 * HD] = total
        held[at, 2 * HD:2 * HD + TILE] = terms
        copy(at, 1).start()
        total = total + own_ref[at, HD:2 * HD]
    for at in range(devices):
        for late in range(2):
            copy(at, late).wait()


def scan(spot, own, local):
    whole = pl.BlockSpec(memory_space=pltpu.VMEM)
    shape = (own.shape[0], 2 * HD + TILE, HD)
    return pl.pallas_call(
        scan_kernel,
        in_specs=[pl.BlockSpec(memory_space=pltpu.SMEM), whole, pl.BlockSpec(memory_space=pltpu.HBM)],
        out_specs=pl.BlockSpec(memory_space=pltpu.HBM),
        out_shape=pltpu.HBM(shape, jnp.float32),
        scratch_shapes=[
            pltpu.VMEM(shape, jnp.float32),
            pltpu.VMEM((TILE, HD), jnp.float32),
            pltpu.SemaphoreType.DMA((own.shape[0], 2)),
            pltpu.SemaphoreType.DMA,
        ],
        compiler_params=params(12 << 20),
        cost_estimate=cost(3 * own.size, 8 * own.size),
        name="scan",
    )(spot, own, pltpu.with_memory_space_constraint(local, pltpu.HBM))


FAR_HEADS = 4


def far_kernel(scale, gain_ref, k_ref, v_ref, g_ref, part_q_ref, part_k_ref, part_v_ref, state_ref,
               dq_ref, dk_ref, dv_ref):
    for j in range(FAR_HEADS):
        columns = slice(j * HD, (j + 1) * HD)
        factor = gain_ref[pl.program_id(0) * FAR_HEADS + j] * scale
        at = pl.program_id(0) * FAR_HEADS + j
        prior = parted(state_ref[at, 0:HD])
        later = parted(state_ref[at, HD:2 * HD])
        dq = part_q_ref[:, columns] + times_transposed(g_ref[:, columns], prior)
        dq_ref[:, columns] = (dq * factor).astype(jnp.bfloat16)
        dk = part_k_ref[:, columns] + times_transposed(v_ref[:, columns], later)
        dk_ref[:, columns] = (dk * factor).astype(jnp.bfloat16)
        dv = part_v_ref[:, columns] + times(k_ref[:, columns], later)
        dv_ref[:, columns] = (dv * factor).astype(jnp.bfloat16)


def far(scale, gain, k, v, g, parts, states):
    _, length, features = k.shape
    wide = pl.BlockSpec((None, length, FAR_HEADS * HD), lambda i: (0, 0, i))
    state = pl.BlockSpec(memory_space=pltpu.VMEM)
    k, v, g, *parts = (pltpu.with_memory_space_constraint(x, pltpu.HBM) for x in (k, v, g, *parts))
    return pl.pallas_call(
        functools.partial(far_kernel, scale),
        grid=(H // FAR_HEADS,),
        in_specs=[pl.BlockSpec(memory_space=pltpu.SMEM)] + [wide] * 6 + [state],
        out_specs=[wide] * 3,
        out_shape=[jax.ShapeDtypeStruct((1, length, features), jnp.bfloat16)] * 3,
        compiler_params=params(40 << 20),
        cost_estimate=cost(12 * length * H * HD * HD, 24 * length * H * HD),
        name="far",
    )(gain, k, v, g, *parts, states)


def exchange(block, axis):
    return lax.all_to_all(block, axis, 0, 0, tiled=True)


def on_device(queries, keys, values, grad_out, node_ids, flags, gain):
    length = queries.shape[1]
    scale = 1.0 / math.sqrt(HD * length * lax.axis_size("ctx"))
    spot = lax.axis_index("ctx").astype(jnp.int32)[None]

    inputs = (queries, keys, values, grad_out)
    owned = exchange(own_states(*inputs), "ctx")
    part_q, local = near(near_q_kernel, inputs, node_ids, flags, 1, 1, "near_q")
    part_k, part_v = near(near_kv_kernel, inputs, node_ids, flags, 2, 0, "near_kv")
    states = exchange(scan(spot, owned, local), "ctx")

    terms = jnp.sum(states[:, 2 * HD:, :], axis=0)
    terms = exchange(jnp.broadcast_to(terms, (lax.axis_size("dp"), TILE, HD)), "dp")
    norm_tokens = lax.axis_size("dp") * length * lax.axis_size("ctx") * HD
    grad_gain = jnp.sum(terms, axis=0)[0, :H] * scale / math.sqrt(norm_tokens)

    return (*far(scale, gain, keys, values, grad_out, (part_q, part_k, part_v), states), grad_gain)


def solution(mesh):
    placed = (
        P("dp", "ctx", None),
        P("dp", "ctx", None),
        P("dp", "ctx", None),
        P("dp", "ctx", None),
        P("dp", "ctx"),
        P("dp", "ctx"),
        P(),
    )
    return jax.shard_map(
        on_device,
        mesh=mesh,
        in_specs=placed,
        out_specs=(P("dp", "ctx", None), P("dp", "ctx", None), P("dp", "ctx", None), P()),
        check_vma=False,
    )
```

```python
import functools
import math

import jax
import jax.numpy as jnp
from jax import lax
from jax.experimental import pallas as pl
from jax.experimental.pallas import tpu as pltpu
from jax.sharding import PartitionSpec as P

H = 16
HD = 128
BLOCK = 128
TILE = 8


def dot(a, b, dims):
    return lax.dot_general(a, b, (dims, ((), ())), preferred_element_type=jnp.float32)


def over_rows(a, b):
    return dot(a, b, ((0,), (0,)))


def over_cols(a, b):
    return dot(a, b, ((1,), (1,)))


def plain(a, b):
    return dot(a, b, ((1,), (0,)))


def head(ref, j, rows=slice(None)):
    return ref[rows, j * HD:(j + 1) * HD]


def parted(state):
    high = state.astype(jnp.bfloat16)
    return high, (state - high.astype(jnp.float32)).astype(jnp.bfloat16)


def times_transposed(rows, parts):
    return over_cols(jnp.concatenate([rows, rows], axis=1), jnp.concatenate(parts, axis=1))


def times(rows, parts):
    return plain(jnp.concatenate([rows, rows], axis=1), jnp.concatenate(parts, axis=0))


def cost(flops, bytes_accessed):
    return pl.CostEstimate(flops=flops, bytes_accessed=bytes_accessed, transcendentals=0)


FULL = 60 * 1024 * 1024


def params(vmem):
    return pltpu.CompilerParams(vmem_limit_bytes=vmem)


CHUNKS = 4


def state_kernel(*refs):
    sources, out_ref, kept, sems = refs[:4], refs[4], refs[5:9], refs[9]
    wide = sources[0].shape[2] // CHUNKS
    heads = wide // HD

    def copy(i, n):
        columns = slice(n * wide, (n + 1) * wide)
        return pltpu.make_async_copy(
            sources[i].at[0, :, columns], kept[i].at[:, columns], sems.at[i, n]
        )

    for n in range(CHUNKS):
        for i in range(4):
            copy(i, n).start()
    for n in range(CHUNKS):
        for i in range(4):
            copy(i, n).wait()
        for j in range(n * heads, (n + 1) * heads):
            q, k, v, g = (head(ref, j) for ref in kept)
            out_ref[j, 0:HD] = over_rows(k, v)
            out_ref[j, HD:2 * HD] = over_rows(q, g)


def own_states(q, k, v, g):
    _, length, features = q.shape
    return pl.pallas_call(
        state_kernel,
        in_specs=[pl.BlockSpec(memory_space=pltpu.HBM)] * 4,
        out_specs=pl.BlockSpec(memory_space=pltpu.VMEM),
        out_shape=jax.ShapeDtypeStruct((H, 2 * HD, HD), jnp.float32),
        scratch_shapes=[pltpu.VMEM((length, features), jnp.bfloat16)] * 4
        + [pltpu.SemaphoreType.DMA((4, CHUNKS))],
        compiler_params=params(FULL),
        cost_estimate=cost(4 * length * H * HD * HD, 8 * length * H * HD),
        name="own_states",
    )(q, k, v, g)


NEAR_HEADS = 2


def summed(block):
    return jnp.sum(jnp.sum(block, axis=0, keepdims=True), axis=1, keepdims=True)


def rows_of(b):
    return slice(b * BLOCK, (b + 1) * BLOCK)


def visible(nodes_ref, marks_ref, b):
    rows = lax.broadcasted_iota(jnp.int32, (BLOCK, BLOCK), 0)
    cols = lax.broadcasted_iota(jnp.int32, (BLOCK, BLOCK), 1)
    across = jnp.broadcast_to(nodes_ref[0:1, rows_of(b)], (BLOCK, BLOCK))
    marks = jnp.broadcast_to(marks_ref[0:1, rows_of(b)], (BLOCK, BLOCK))
    return ((cols <= rows) & ((across == across.T) | (marks == 1))).astype(jnp.float32)


def near_kernel(count, q_ref, k_ref, v_ref, g_ref, nodes_ref, marks_ref,
                dq_ref, dk_ref, dv_ref, term_ref, seen_ref, turned_ref, earlier_ref):
    @pl.when(pl.program_id(0) == 0)
    def _():
        for b in range(count):
            seen_ref[b] = visible(nodes_ref, marks_ref, b)
            turned_ref[b] = visible(nodes_ref, marks_ref, b).T
        term_ref[...] = jnp.zeros_like(term_ref)

    heads = range(NEAR_HEADS)

    def loaded(ref, b):
        return [head(ref, j, rows_of(b)) for j in heads]

    def store(ref, b, values):
        for j in heads:
            ref[rows_of(b), j * HD:(j + 1) * HD] = values[j].astype(jnp.bfloat16)

    earlier = None
    for b in range(count):
        k, v, g = (loaded(ref, b) for ref in (k_ref, v_ref, g_ref))
        dscores = [(over_cols(g[j], v[j]) * seen_ref[b]).astype(jnp.bfloat16) for j in heads]
        kv = [over_rows(k[j], v[j]) for j in heads] if b < count - 1 else None
        dq = [plain(dscores[j], k[j]) for j in heads]
        if earlier is not None:
            dq = [dq[j] + times_transposed(g[j], parted(earlier[j])) for j in heads]
            for j in heads:
                earlier_ref[j, b] = earlier[j]
        store(dq_ref, b, dq)
        if kv is not None:
            earlier = kv if earlier is None else [earlier[j] + kv[j] for j in heads]

    later = None
    term = [jnp.zeros((BLOCK, BLOCK), jnp.float32) for j in heads]
    for b in reversed(range(count)):
        q, k, v, g = (loaded(ref, b) for ref in (q_ref, k_ref, v_ref, g_ref))
        scores = [over_cols(k[j], q[j]) * turned_ref[b] for j in heads]
        dscores = [over_cols(v[j], g[j]) * turned_ref[b] for j in heads]
        qg = [over_rows(q[j], g[j]) for j in heads] if b > 0 else None
        term = [term[j] + scores[j] * dscores[j] for j in heads]
        dk = [plain(dscores[j].astype(jnp.bfloat16), q[j]) for j in heads]
        dv = [plain(scores[j].astype(jnp.bfloat16), g[j]) for j in heads]
        if later is not None:
            parts = [parted(later[j]) for j in heads]
            dk = [dk[j] + times_transposed(v[j], parts[j]) for j in heads]
            dv = [dv[j] + times(k[j], parts[j]) for j in heads]
        store(dk_ref, b, dk)
        store(dv_ref, b, dv)
        if qg is not None:
            term = [term[j] + earlier_ref[j, b] * qg[j] for j in heads]
            later = qg if later is None else [later[j] + qg[j] for j in heads]

    lanes = lax.broadcasted_iota(jnp.int32, (TILE, HD), 1)
    for j in heads:
        here = lanes == pl.program_id(0) * NEAR_HEADS + j
        term_ref[...] += jnp.where(here, summed(term[j]), 0.0)


def near(inputs, nodes, marks):
    _, length, features = inputs[0].shape
    count = length // BLOCK
    wide = pl.BlockSpec((None, length, NEAR_HEADS * HD), lambda i: (0, 0, i))
    flat = pl.BlockSpec((1, length), lambda i: (0, 0))
    masks = pltpu.VMEM((count, BLOCK, BLOCK), jnp.float32)
    return pl.pallas_call(
        functools.partial(near_kernel, count),
        grid=(H // NEAR_HEADS,),
        in_specs=[wide] * 4 + [flat] * 2,
        out_specs=[wide] * 3 + [pl.BlockSpec((TILE, HD), lambda i: (0, 0))],
        out_shape=[jax.ShapeDtypeStruct((1, length, features), jnp.bfloat16)] * 3
        + [jax.ShapeDtypeStruct((TILE, HD), jnp.float32)],
        scratch_shapes=[masks, masks, pltpu.VMEM((NEAR_HEADS, count, BLOCK, BLOCK), jnp.float32)],
        compiler_params=params(FULL),
        cost_estimate=cost(28 * length * H * HD * HD, 14 * length * H * HD),
        name="near",
    )(*inputs, nodes, marks)


def scan_kernel(spot_ref, own_ref, local_ref, out_ref, held, gained, sems, sem):
    devices = own_ref.shape[0]
    local = pltpu.make_async_copy(local_ref, gained, sem)
    local.start()

    def copy(at, late):
        rows = slice(HD, 2 * HD + TILE) if late else slice(0, HD)
        return pltpu.make_async_copy(held.at[at, rows], out_ref.at[at, rows], sems.at[at, late])

    total = jnp.zeros((HD, HD), jnp.float32)
    cross = jnp.zeros((HD, HD), jnp.float32)
    for at in range(devices):
        held[at, 0:HD] = total
        copy(at, 0).start()
        cross = cross + total * own_ref[at, HD:2 * HD]
        total = total + own_ref[at, 0:HD]
    lanes = lax.broadcasted_iota(jnp.int32, (TILE, HD), 1)
    local.wait()
    terms = gained[...] + jnp.where(lanes == spot_ref[0], summed(cross), 0.0)
    total = jnp.zeros((HD, HD), jnp.float32)
    for at in reversed(range(devices)):
        held[at, HD:2 * HD] = total
        held[at, 2 * HD:2 * HD + TILE] = terms
        copy(at, 1).start()
        total = total + own_ref[at, HD:2 * HD]
    for at in range(devices):
        for late in range(2):
            copy(at, late).wait()


def scan(spot, own, local):
    whole = pl.BlockSpec(memory_space=pltpu.VMEM)
    shape = (own.shape[0], 2 * HD + TILE, HD)
    return pl.pallas_call(
        scan_kernel,
        in_specs=[pl.BlockSpec(memory_space=pltpu.SMEM), whole, pl.BlockSpec(memory_space=pltpu.HBM)],
        out_specs=pl.BlockSpec(memory_space=pltpu.HBM),
        out_shape=pltpu.HBM(shape, jnp.float32),
        scratch_shapes=[
            pltpu.VMEM(shape, jnp.float32),
            pltpu.VMEM((TILE, HD), jnp.float32),
            pltpu.SemaphoreType.DMA((own.shape[0], 2)),
            pltpu.SemaphoreType.DMA,
        ],
        compiler_params=params(12 << 20),
        cost_estimate=cost(3 * own.size, 8 * own.size),
        name="scan",
    )(spot, own, pltpu.with_memory_space_constraint(local, pltpu.HBM))


FAR_HEADS = 4


def far_kernel(scale, gain_ref, k_ref, v_ref, g_ref, part_q_ref, part_k_ref, part_v_ref, state_ref,
               dq_ref, dk_ref, dv_ref):
    for j in range(FAR_HEADS):
        columns = slice(j * HD, (j + 1) * HD)
        factor = gain_ref[pl.program_id(0) * FAR_HEADS + j] * scale
        at = pl.program_id(0) * FAR_HEADS + j
        prior = parted(state_ref[at, 0:HD])
        later = parted(state_ref[at, HD:2 * HD])
        dq = part_q_ref[:, columns] + times_transposed(g_ref[:, columns], prior)
        dq_ref[:, columns] = (dq * factor).astype(jnp.bfloat16)
        dk = part_k_ref[:, columns] + times_transposed(v_ref[:, columns], later)
        dk_ref[:, columns] = (dk * factor).astype(jnp.bfloat16)
        dv = part_v_ref[:, columns] + times(k_ref[:, columns], later)
        dv_ref[:, columns] = (dv * factor).astype(jnp.bfloat16)


def far(scale, gain, k, v, g, parts, states):
    _, length, features = k.shape
    wide = pl.BlockSpec((None, length, FAR_HEADS * HD), lambda i: (0, 0, i))
    state = pl.BlockSpec(memory_space=pltpu.VMEM)
    k, v, g, *parts = (pltpu.with_memory_space_constraint(x, pltpu.HBM) for x in (k, v, g, *parts))
    return pl.pallas_call(
        functools.partial(far_kernel, scale),
        grid=(H // FAR_HEADS,),
        in_specs=[pl.BlockSpec(memory_space=pltpu.SMEM)] + [wide] * 6 + [state],
        out_specs=[wide] * 3,
        out_shape=[jax.ShapeDtypeStruct((1, length, features), jnp.bfloat16)] * 3,
        compiler_params=params(40 << 20),
        cost_estimate=cost(12 * length * H * HD * HD, 24 * length * H * HD),
        name="far",
    )(gain, k, v, g, *parts, states)


def exchange(block, axis):
    return lax.all_to_all(block, axis, 0, 0, tiled=True)


def on_device(queries, keys, values, grad_out, node_ids, flags, gain):
    length = queries.shape[1]
    scale = 1.0 / math.sqrt(HD * length * lax.axis_size("ctx"))
    spot = lax.axis_index("ctx").astype(jnp.int32)[None]

    inputs = (queries, keys, values, grad_out)
    owned = exchange(own_states(*inputs), "ctx")
    *parts, local = near(inputs, node_ids, flags)
    states = exchange(scan(spot, owned, local), "ctx")

    terms = jnp.sum(states[:, 2 * HD:, :], axis=0)
    terms = exchange(jnp.broadcast_to(terms, (lax.axis_size("dp"), TILE, HD)), "dp")
    norm_tokens = lax.axis_size("dp") * length * lax.axis_size("ctx") * HD
    grad_gain = jnp.sum(terms, axis=0)[0, :H] * scale / math.sqrt(norm_tokens)

    return (*far(scale, gain, keys, values, grad_out, parts, states), grad_gain)


def solution(mesh):
    placed = (
        P("dp", "ctx", None),
        P("dp", "ctx", None),
        P("dp", "ctx", None),
        P("dp", "ctx", None),
        P("dp", "ctx"),
        P("dp", "ctx"),
        P(),
    )
    return jax.shard_map(
        on_device,
        mesh=mesh,
        in_specs=placed,
        out_specs=(P("dp", "ctx", None), P("dp", "ctx", None), P("dp", "ctx", None), P()),
        check_vma=False,
    )
```

```python
import functools
import math

import jax
import jax.numpy as jnp
from jax import lax
from jax.experimental import pallas as pl
from jax.experimental.pallas import tpu as pltpu
from jax.sharding import PartitionSpec as P

H = 16
HD = 128
BLOCK = 128
TILE = 8


def dot(a, b, dims):
    return lax.dot_general(a, b, (dims, ((), ())), preferred_element_type=jnp.float32)


def over_rows(a, b):
    return dot(a, b, ((0,), (0,)))


def over_cols(a, b):
    return dot(a, b, ((1,), (1,)))


def plain(a, b):
    return dot(a, b, ((1,), (0,)))


def head(ref, j, rows=slice(None)):
    return ref[rows, j * HD:(j + 1) * HD]


def parted(state):
    high = state.astype(jnp.bfloat16)
    return high, (state - high.astype(jnp.float32)).astype(jnp.bfloat16)


def times_transposed(rows, parts):
    return over_cols(jnp.concatenate([rows, rows], axis=1), jnp.concatenate(parts, axis=1))


def times(rows, parts):
    return plain(jnp.concatenate([rows, rows], axis=1), jnp.concatenate(parts, axis=0))


def cost(flops, bytes_accessed):
    return pl.CostEstimate(flops=flops, bytes_accessed=bytes_accessed, transcendentals=0)


FULL = 60 * 1024 * 1024


def params(vmem):
    return pltpu.CompilerParams(vmem_limit_bytes=vmem)


CHUNKS = 8


def state_kernel(*refs):
    sources, out_ref, kept, held, sems, out_sems = refs[:4], refs[4], refs[5:9], refs[9], refs[10], refs[11]
    wide = sources[0].shape[2] // CHUNKS
    heads = wide // HD

    def copy(i, n):
        columns = slice(n * wide, (n + 1) * wide)
        return pltpu.make_async_copy(
            sources[i].at[0, :, columns], kept[i].at[:, columns], sems.at[i, n]
        )

    def result(n):
        part = slice(n * heads, (n + 1) * heads)
        return pltpu.make_async_copy(held.at[part], out_ref.at[part], out_sems.at[n])

    for n in range(CHUNKS):
        for i in range(4):
            copy(i, n).start()
    for n in range(CHUNKS):
        for i in range(4):
            copy(i, n).wait()
        for j in range(n * heads, (n + 1) * heads):
            q, k, v, g = (head(ref, j) for ref in kept)
            both = over_rows(jnp.concatenate([k, q], axis=1), jnp.concatenate([v, g], axis=1))
            held[j, 0:HD] = both[:HD, :HD]
            held[j, HD:2 * HD] = both[HD:, HD:]
        result(n).start()
    for n in range(CHUNKS):
        result(n).wait()


def own_states(q, k, v, g):
    _, length, features = q.shape
    return pl.pallas_call(
        state_kernel,
        in_specs=[pl.BlockSpec(memory_space=pltpu.HBM)] * 4,
        out_specs=pl.BlockSpec(memory_space=pltpu.HBM),
        out_shape=pltpu.HBM((H, 2 * HD, HD), jnp.float32),
        scratch_shapes=[pltpu.VMEM((length, features), jnp.bfloat16)] * 4
        + [
            pltpu.VMEM((H, 2 * HD, HD), jnp.float32),
            pltpu.SemaphoreType.DMA((4, CHUNKS)),
            pltpu.SemaphoreType.DMA((CHUNKS,)),
        ],
        compiler_params=params(FULL),
        cost_estimate=cost(4 * length * H * HD * HD, 8 * length * H * HD),
        name="own_states",
    )(q, k, v, g)


NEAR_HEADS = 2


def summed(block):
    return jnp.sum(jnp.sum(block, axis=0, keepdims=True), axis=1, keepdims=True)


def rows_of(b):
    return slice(b * BLOCK, (b + 1) * BLOCK)


def visible(nodes_ref, marks_ref, b):
    rows = lax.broadcasted_iota(jnp.int32, (BLOCK, BLOCK), 0)
    cols = lax.broadcasted_iota(jnp.int32, (BLOCK, BLOCK), 1)
    across = jnp.broadcast_to(nodes_ref[0:1, rows_of(b)], (BLOCK, BLOCK))
    marks = jnp.broadcast_to(marks_ref[0:1, rows_of(b)], (BLOCK, BLOCK))
    return ((cols <= rows) & ((across == across.T) | (marks == 1))).astype(jnp.float32)


def near_kernel(count, q_ref, k_ref, v_ref, g_ref, nodes_ref, marks_ref,
                dq_ref, dk_ref, dv_ref, term_ref, seen_ref, turned_ref, earlier_ref):
    @pl.when(pl.program_id(0) == 0)
    def _():
        for b in range(count):
            seen_ref[b] = visible(nodes_ref, marks_ref, b)
            turned_ref[b] = visible(nodes_ref, marks_ref, b).T
        term_ref[...] = jnp.zeros_like(term_ref)

    heads = range(NEAR_HEADS)

    def loaded(ref, b):
        return [head(ref, j, rows_of(b)) for j in heads]

    def store(ref, b, values):
        for j in heads:
            ref[rows_of(b), j * HD:(j + 1) * HD] = values[j].astype(jnp.bfloat16)

    earlier = None
    for b in range(count):
        k, v, g = (loaded(ref, b) for ref in (k_ref, v_ref, g_ref))
        dscores = [(over_cols(g[j], v[j]) * seen_ref[b]).astype(jnp.bfloat16) for j in heads]
        kv = [over_rows(k[j], v[j]) for j in heads] if b < count - 1 else None
        dq = [plain(dscores[j], k[j]) for j in heads]
        if earlier is not None:
            dq = [dq[j] + times_transposed(g[j], parted(earlier[j])) for j in heads]
            for j in heads:
                earlier_ref[j, b] = earlier[j]
        store(dq_ref, b, dq)
        if kv is not None:
            earlier = kv if earlier is None else [earlier[j] + kv[j] for j in heads]

    later = None
    term = [jnp.zeros((BLOCK, BLOCK), jnp.float32) for j in heads]
    for b in reversed(range(count)):
        q, k, v, g = (loaded(ref, b) for ref in (q_ref, k_ref, v_ref, g_ref))
        scores = [over_cols(k[j], q[j]) * turned_ref[b] for j in heads]
        dscores = [over_cols(v[j], g[j]) * turned_ref[b] for j in heads]
        qg = [over_rows(q[j], g[j]) for j in heads] if b > 0 else None
        term = [term[j] + scores[j] * dscores[j] for j in heads]
        dk = [plain(dscores[j].astype(jnp.bfloat16), q[j]) for j in heads]
        dv = [plain(scores[j].astype(jnp.bfloat16), g[j]) for j in heads]
        if later is not None:
            parts = [parted(later[j]) for j in heads]
            dk = [dk[j] + times_transposed(v[j], parts[j]) for j in heads]
            dv = [dv[j] + times(k[j], parts[j]) for j in heads]
        store(dk_ref, b, dk)
        store(dv_ref, b, dv)
        if qg is not None:
            term = [term[j] + earlier_ref[j, b] * qg[j] for j in heads]
            later = qg if later is None else [later[j] + qg[j] for j in heads]

    lanes = lax.broadcasted_iota(jnp.int32, (TILE, HD), 1)
    for j in heads:
        here = lanes == pl.program_id(0) * NEAR_HEADS + j
        term_ref[...] += jnp.where(here, summed(term[j]), 0.0)


def near(inputs, nodes, marks):
    _, length, features = inputs[0].shape
    count = length // BLOCK
    wide = pl.BlockSpec((None, length, NEAR_HEADS * HD), lambda i: (0, 0, i))
    flat = pl.BlockSpec((1, length), lambda i: (0, 0))
    masks = pltpu.VMEM((count, BLOCK, BLOCK), jnp.float32)
    return pl.pallas_call(
        functools.partial(near_kernel, count),
        grid=(H // NEAR_HEADS,),
        in_specs=[wide] * 4 + [flat] * 2,
        out_specs=[wide] * 3 + [pl.BlockSpec((TILE, HD), lambda i: (0, 0))],
        out_shape=[jax.ShapeDtypeStruct((1, length, features), jnp.bfloat16)] * 3
        + [jax.ShapeDtypeStruct((TILE, HD), jnp.float32)],
        scratch_shapes=[masks, masks, pltpu.VMEM((NEAR_HEADS, count, BLOCK, BLOCK), jnp.float32)],
        compiler_params=params(FULL),
        cost_estimate=cost(28 * length * H * HD * HD, 14 * length * H * HD),
        name="near",
    )(*inputs, nodes, marks)


def scan_kernel(spot_ref, own_ref, local_ref, out_ref, held, gained, sems, sem):
    devices = own_ref.shape[0]
    local = pltpu.make_async_copy(local_ref, gained, sem)
    local.start()

    def copy(at, late):
        rows = slice(HD, 2 * HD + TILE) if late else slice(0, HD)
        return pltpu.make_async_copy(held.at[at, rows], out_ref.at[at, rows], sems.at[at, late])

    total = jnp.zeros((HD, HD), jnp.float32)
    cross = jnp.zeros((HD, HD), jnp.float32)
    for at in range(devices):
        held[at, 0:HD] = total
        copy(at, 0).start()
        cross = cross + total * own_ref[at, HD:2 * HD]
        total = total + own_ref[at, 0:HD]
    lanes = lax.broadcasted_iota(jnp.int32, (TILE, HD), 1)
    local.wait()
    terms = gained[...] + jnp.where(lanes == spot_ref[0], summed(cross), 0.0)
    total = jnp.zeros((HD, HD), jnp.float32)
    for at in reversed(range(devices)):
        held[at, HD:2 * HD] = total
        held[at, 2 * HD:2 * HD + TILE] = terms
        copy(at, 1).start()
        total = total + own_ref[at, HD:2 * HD]
    for at in range(devices):
        for late in range(2):
            copy(at, late).wait()


def scan(spot, own, local):
    whole = pl.BlockSpec(memory_space=pltpu.VMEM)
    shape = (own.shape[0], 2 * HD + TILE, HD)
    return pl.pallas_call(
        scan_kernel,
        in_specs=[pl.BlockSpec(memory_space=pltpu.SMEM), whole, pl.BlockSpec(memory_space=pltpu.HBM)],
        out_specs=pl.BlockSpec(memory_space=pltpu.HBM),
        out_shape=pltpu.HBM(shape, jnp.float32),
        scratch_shapes=[
            pltpu.VMEM(shape, jnp.float32),
            pltpu.VMEM((TILE, HD), jnp.float32),
            pltpu.SemaphoreType.DMA((own.shape[0], 2)),
            pltpu.SemaphoreType.DMA,
        ],
        compiler_params=params(12 << 20),
        cost_estimate=cost(3 * own.size, 8 * own.size),
        name="scan",
    )(spot, own, pltpu.with_memory_space_constraint(local, pltpu.HBM))


FAR_HEADS = 4


def far_kernel(scale, gain_ref, k_ref, v_ref, g_ref, part_q_ref, part_k_ref, part_v_ref, state_ref,
               dq_ref, dk_ref, dv_ref):
    for j in range(FAR_HEADS):
        columns = slice(j * HD, (j + 1) * HD)
        factor = gain_ref[pl.program_id(0) * FAR_HEADS + j] * scale
        at = pl.program_id(0) * FAR_HEADS + j
        prior = parted(state_ref[at, 0:HD])
        later = parted(state_ref[at, HD:2 * HD])
        dq = part_q_ref[:, columns] + times_transposed(g_ref[:, columns], prior)
        dq_ref[:, columns] = (dq * factor).astype(jnp.bfloat16)
        dk = part_k_ref[:, columns] + times_transposed(v_ref[:, columns], later)
        dk_ref[:, columns] = (dk * factor).astype(jnp.bfloat16)
        dv = part_v_ref[:, columns] + times(k_ref[:, columns], later)
        dv_ref[:, columns] = (dv * factor).astype(jnp.bfloat16)


def far(scale, gain, k, v, g, parts, states):
    _, length, features = k.shape
    wide = pl.BlockSpec((None, length, FAR_HEADS * HD), lambda i: (0, 0, i))
    state = pl.BlockSpec(memory_space=pltpu.VMEM)
    k, v, g, *parts = (pltpu.with_memory_space_constraint(x, pltpu.HBM) for x in (k, v, g, *parts))
    return pl.pallas_call(
        functools.partial(far_kernel, scale),
        grid=(H // FAR_HEADS,),
        in_specs=[pl.BlockSpec(memory_space=pltpu.SMEM)] + [wide] * 6 + [state],
        out_specs=[wide] * 3,
        out_shape=[jax.ShapeDtypeStruct((1, length, features), jnp.bfloat16)] * 3,
        compiler_params=params(40 << 20),
        cost_estimate=cost(12 * length * H * HD * HD, 24 * length * H * HD),
        name="far",
    )(gain, k, v, g, *parts, states)


def exchange(block, axis):
    return lax.all_to_all(block, axis, 0, 0, tiled=True)


def on_device(queries, keys, values, grad_out, node_ids, flags, gain):
    length = queries.shape[1]
    scale = 1.0 / math.sqrt(HD * length * lax.axis_size("ctx"))
    spot = lax.axis_index("ctx").astype(jnp.int32)[None]

    inputs = (queries, keys, values, grad_out)
    owned = exchange(own_states(*inputs), "ctx")
    *parts, local = near(inputs, node_ids, flags)
    states = exchange(scan(spot, owned, local), "ctx")

    terms = jnp.sum(states[:, 2 * HD:, :], axis=0)
    terms = exchange(jnp.broadcast_to(terms, (lax.axis_size("dp"), TILE, HD)), "dp")
    norm_tokens = lax.axis_size("dp") * length * lax.axis_size("ctx") * HD
    grad_gain = jnp.sum(terms, axis=0)[0, :H] * scale / math.sqrt(norm_tokens)

    return (*far(scale, gain, keys, values, grad_out, parts, states), grad_gain)


def solution(mesh):
    placed = (
        P("dp", "ctx", None),
        P("dp", "ctx", None),
        P("dp", "ctx", None),
        P("dp", "ctx", None),
        P("dp", "ctx"),
        P("dp", "ctx"),
        P(),
    )
    return jax.shard_map(
        on_device,
        mesh=mesh,
        in_specs=placed,
        out_specs=(P("dp", "ctx", None), P("dp", "ctx", None), P("dp", "ctx", None), P()),
        check_vma=False,
    )
```

```python
import functools
import math

import jax
import jax.numpy as jnp
from jax import lax
from jax.experimental import pallas as pl
from jax.experimental.pallas import tpu as pltpu
from jax.sharding import PartitionSpec as P

H = 16
HD = 128
BLOCK = 128
TILE = 8


def dot(a, b, dims):
    return lax.dot_general(a, b, (dims, ((), ())), preferred_element_type=jnp.float32)


def over_rows(a, b):
    return dot(a, b, ((0,), (0,)))


def over_cols(a, b):
    return dot(a, b, ((1,), (1,)))


def plain(a, b):
    return dot(a, b, ((1,), (0,)))


def head(ref, j, rows=slice(None)):
    return ref[rows, j * HD:(j + 1) * HD]


def parted(state):
    high = state.astype(jnp.bfloat16)
    return high, (state - high.astype(jnp.float32)).astype(jnp.bfloat16)


def times_transposed(rows, parts):
    return over_cols(jnp.concatenate([rows, rows], axis=1), jnp.concatenate(parts, axis=1))


def times(rows, parts):
    return plain(jnp.concatenate([rows, rows], axis=1), jnp.concatenate(parts, axis=0))


def cost(flops, bytes_accessed):
    return pl.CostEstimate(flops=flops, bytes_accessed=bytes_accessed, transcendentals=0)


FULL = 60 * 1024 * 1024


def params(vmem):
    return pltpu.CompilerParams(vmem_limit_bytes=vmem)


CHUNKS = 4


def state_kernel(*refs):
    sources, out_ref, kept, held, sems, out_sems = refs[:4], refs[4], refs[5:9], refs[9], refs[10], refs[11]
    wide = sources[0].shape[2] // CHUNKS
    heads = wide // HD

    def copy(i, n):
        columns = slice(n * wide, (n + 1) * wide)
        return pltpu.make_async_copy(
            sources[i].at[0, :, columns], kept[i].at[:, columns], sems.at[i, n]
        )

    def result(n):
        part = slice(n * heads, (n + 1) * heads)
        return pltpu.make_async_copy(held.at[part], out_ref.at[part], out_sems.at[n])

    for n in range(CHUNKS):
        for i in range(4):
            copy(i, n).start()
    for n in range(CHUNKS):
        for i in range(4):
            copy(i, n).wait()
        for j in range(n * heads, (n + 1) * heads):
            q, k, v, g = (head(ref, j) for ref in kept)
            both = over_rows(jnp.concatenate([k, q], axis=1), jnp.concatenate([v, g], axis=1))
            held[j, 0:HD] = both[:HD, :HD]
            held[j, HD:2 * HD] = both[HD:, HD:]
        result(n).start()
    for n in range(CHUNKS):
        result(n).wait()


def own_states(q, k, v, g):
    _, length, features = q.shape
    return pl.pallas_call(
        state_kernel,
        in_specs=[pl.BlockSpec(memory_space=pltpu.HBM)] * 4,
        out_specs=pl.BlockSpec(memory_space=pltpu.HBM),
        out_shape=pltpu.HBM((H, 2 * HD, HD), jnp.float32),
        scratch_shapes=[pltpu.VMEM((length, features), jnp.bfloat16)] * 4
        + [
            pltpu.VMEM((H, 2 * HD, HD), jnp.float32),
            pltpu.SemaphoreType.DMA((4, CHUNKS)),
            pltpu.SemaphoreType.DMA((CHUNKS,)),
        ],
        compiler_params=params(FULL),
        cost_estimate=cost(4 * length * H * HD * HD, 8 * length * H * HD),
        name="own_states",
    )(q, k, v, g)


NEAR_HEADS = 2


def summed(block):
    return jnp.sum(jnp.sum(block, axis=0, keepdims=True), axis=1, keepdims=True)


def rows_of(b):
    return slice(b * BLOCK, (b + 1) * BLOCK)


def visible(nodes_ref, marks_ref, b):
    rows = lax.broadcasted_iota(jnp.int32, (BLOCK, BLOCK), 0)
    cols = lax.broadcasted_iota(jnp.int32, (BLOCK, BLOCK), 1)
    across = jnp.broadcast_to(nodes_ref[0:1, rows_of(b)], (BLOCK, BLOCK))
    marks = jnp.broadcast_to(marks_ref[0:1, rows_of(b)], (BLOCK, BLOCK))
    return ((cols <= rows) & ((across == across.T) | (marks == 1))).astype(jnp.float32)


def near_kernel(count, q_ref, k_ref, v_ref, g_ref, nodes_ref, marks_ref,
                dq_ref, dk_ref, dv_ref, term_ref, seen_ref, turned_ref, earlier_ref):
    @pl.when(pl.program_id(0) == 0)
    def _():
        for b in range(count):
            seen_ref[b] = visible(nodes_ref, marks_ref, b)
            turned_ref[b] = visible(nodes_ref, marks_ref, b).T
        term_ref[...] = jnp.zeros_like(term_ref)

    heads = range(NEAR_HEADS)

    def loaded(ref, b):
        return [head(ref, j, rows_of(b)) for j in heads]

    def store(ref, b, values):
        for j in heads:
            ref[rows_of(b), j * HD:(j + 1) * HD] = values[j].astype(jnp.bfloat16)

    earlier = None
    for b in range(count):
        k, v, g = (loaded(ref, b) for ref in (k_ref, v_ref, g_ref))
        dscores = [(over_cols(g[j], v[j]) * seen_ref[b]).astype(jnp.bfloat16) for j in heads]
        kv = [over_rows(k[j], v[j]) for j in heads] if b < count - 1 else None
        dq = [plain(dscores[j], k[j]) for j in heads]
        if earlier is not None:
            dq = [dq[j] + times_transposed(g[j], parted(earlier[j])) for j in heads]
            for j in heads:
                earlier_ref[j, b] = earlier[j]
        store(dq_ref, b, dq)
        if kv is not None:
            earlier = kv if earlier is None else [earlier[j] + kv[j] for j in heads]

    later = None
    term = [jnp.zeros((BLOCK, BLOCK), jnp.float32) for j in heads]
    for b in reversed(range(count)):
        q, k, v, g = (loaded(ref, b) for ref in (q_ref, k_ref, v_ref, g_ref))
        scores = [over_cols(k[j], q[j]) * turned_ref[b] for j in heads]
        dscores = [over_cols(v[j], g[j]) * turned_ref[b] for j in heads]
        qg = [over_rows(q[j], g[j]) for j in heads] if b > 0 else None
        term = [term[j] + scores[j] * dscores[j] for j in heads]
        dk = [plain(dscores[j].astype(jnp.bfloat16), q[j]) for j in heads]
        dv = [plain(scores[j].astype(jnp.bfloat16), g[j]) for j in heads]
        if later is not None:
            parts = [parted(later[j]) for j in heads]
            dk = [dk[j] + times_transposed(v[j], parts[j]) for j in heads]
            dv = [dv[j] + times(k[j], parts[j]) for j in heads]
        store(dk_ref, b, dk)
        store(dv_ref, b, dv)
        if qg is not None:
            term = [term[j] + earlier_ref[j, b] * qg[j] for j in heads]
            later = qg if later is None else [later[j] + qg[j] for j in heads]

    lanes = lax.broadcasted_iota(jnp.int32, (TILE, HD), 1)
    for j in heads:
        here = lanes == pl.program_id(0) * NEAR_HEADS + j
        term_ref[...] += jnp.where(here, summed(term[j]), 0.0)


def near(inputs, nodes, marks):
    _, length, features = inputs[0].shape
    count = length // BLOCK
    wide = pl.BlockSpec((None, length, NEAR_HEADS * HD), lambda i: (0, 0, i))
    flat = pl.BlockSpec((1, length), lambda i: (0, 0))
    masks = pltpu.VMEM((count, BLOCK, BLOCK), jnp.float32)
    return pl.pallas_call(
        functools.partial(near_kernel, count),
        grid=(H // NEAR_HEADS,),
        in_specs=[wide] * 4 + [flat] * 2,
        out_specs=[wide] * 3 + [pl.BlockSpec((TILE, HD), lambda i: (0, 0))],
        out_shape=[jax.ShapeDtypeStruct((1, length, features), jnp.bfloat16)] * 3
        + [jax.ShapeDtypeStruct((TILE, HD), jnp.float32)],
        scratch_shapes=[masks, masks, pltpu.VMEM((NEAR_HEADS, count, BLOCK, BLOCK), jnp.float32)],
        compiler_params=params(FULL),
        cost_estimate=cost(28 * length * H * HD * HD, 14 * length * H * HD),
        name="near",
    )(*inputs, nodes, marks)


def scan_kernel(spot_ref, own_ref, local_ref, out_ref, held, gained, sems, sem):
    devices = own_ref.shape[0]
    local = pltpu.make_async_copy(local_ref, gained, sem)
    local.start()

    def copy(at, late):
        rows = slice(HD, 2 * HD + TILE) if late else slice(0, HD)
        return pltpu.make_async_copy(held.at[at, rows], out_ref.at[at, rows], sems.at[at, late])

    total = jnp.zeros((HD, HD), jnp.float32)
    cross = jnp.zeros((HD, HD), jnp.float32)
    for at in range(devices):
        held[at, 0:HD] = total
        copy(at, 0).start()
        cross = cross + total * own_ref[at, HD:2 * HD]
        total = total + own_ref[at, 0:HD]
    lanes = lax.broadcasted_iota(jnp.int32, (TILE, HD), 1)
    local.wait()
    terms = gained[...] + jnp.where(lanes == spot_ref[0], summed(cross), 0.0)
    total = jnp.zeros((HD, HD), jnp.float32)
    for at in reversed(range(devices)):
        held[at, HD:2 * HD] = total
        held[at, 2 * HD:2 * HD + TILE] = terms
        copy(at, 1).start()
        total = total + own_ref[at, HD:2 * HD]
    for at in range(devices):
        for late in range(2):
            copy(at, late).wait()


def scan(spot, own, local):
    whole = pl.BlockSpec(memory_space=pltpu.VMEM)
    shape = (own.shape[0], 2 * HD + TILE, HD)
    return pl.pallas_call(
        scan_kernel,
        in_specs=[pl.BlockSpec(memory_space=pltpu.SMEM), whole, pl.BlockSpec(memory_space=pltpu.HBM)],
        out_specs=pl.BlockSpec(memory_space=pltpu.HBM),
        out_shape=pltpu.HBM(shape, jnp.float32),
        scratch_shapes=[
            pltpu.VMEM(shape, jnp.float32),
            pltpu.VMEM((TILE, HD), jnp.float32),
            pltpu.SemaphoreType.DMA((own.shape[0], 2)),
            pltpu.SemaphoreType.DMA,
        ],
        compiler_params=params(12 << 20),
        cost_estimate=cost(3 * own.size, 8 * own.size),
        name="scan",
    )(spot, own, pltpu.with_memory_space_constraint(local, pltpu.HBM))


FAR_HEADS = 4


def far_kernel(scale, gain_ref, k_ref, v_ref, g_ref, part_q_ref, part_k_ref, part_v_ref, state_ref,
               dq_ref, dk_ref, dv_ref):
    for j in range(FAR_HEADS):
        columns = slice(j * HD, (j + 1) * HD)
        factor = gain_ref[pl.program_id(0) * FAR_HEADS + j] * scale
        at = pl.program_id(0) * FAR_HEADS + j
        prior = parted(state_ref[at, 0:HD])
        later = parted(state_ref[at, HD:2 * HD])
        dq = part_q_ref[:, columns] + times_transposed(g_ref[:, columns], prior)
        dq_ref[:, columns] = (dq * factor).astype(jnp.bfloat16)
        dk = part_k_ref[:, columns] + times_transposed(v_ref[:, columns], later)
        dk_ref[:, columns] = (dk * factor).astype(jnp.bfloat16)
        dv = part_v_ref[:, columns] + times(k_ref[:, columns], later)
        dv_ref[:, columns] = (dv * factor).astype(jnp.bfloat16)


def far(scale, gain, k, v, g, parts, states):
    _, length, features = k.shape
    wide = pl.BlockSpec((None, length, FAR_HEADS * HD), lambda i: (0, 0, i))
    state = pl.BlockSpec(memory_space=pltpu.VMEM)
    k, v, g, *parts = (pltpu.with_memory_space_constraint(x, pltpu.HBM) for x in (k, v, g, *parts))
    return pl.pallas_call(
        functools.partial(far_kernel, scale),
        grid=(H // FAR_HEADS,),
        in_specs=[pl.BlockSpec(memory_space=pltpu.SMEM)] + [wide] * 6 + [state],
        out_specs=[wide] * 3,
        out_shape=[jax.ShapeDtypeStruct((1, length, features), jnp.bfloat16)] * 3,
        compiler_params=params(40 << 20),
        cost_estimate=cost(12 * length * H * HD * HD, 24 * length * H * HD),
        name="far",
    )(gain, k, v, g, *parts, states)


def gathered_kernel(state_ref, out_ref):
    total = state_ref[0, 2 * HD:2 * HD + TILE]
    for at in range(1, state_ref.shape[0]):
        total = total + state_ref[at, 2 * HD:2 * HD + TILE]
    for at in range(out_ref.shape[0]):
        out_ref[at] = total


def gathered(states, copies):
    whole = pl.BlockSpec(memory_space=pltpu.VMEM)
    return pl.pallas_call(
        gathered_kernel,
        in_specs=[whole],
        out_specs=whole,
        out_shape=jax.ShapeDtypeStruct((copies, TILE, HD), jnp.float32),
        compiler_params=params(4 << 20),
        cost_estimate=cost(states.shape[0] * TILE * HD, 4 * copies * TILE * HD),
        name="gathered",
    )(states)


def exchange(block, axis):
    return lax.all_to_all(block, axis, 0, 0, tiled=True)


def on_device(queries, keys, values, grad_out, node_ids, flags, gain):
    length = queries.shape[1]
    scale = 1.0 / math.sqrt(HD * length * lax.axis_size("ctx"))
    spot = lax.axis_index("ctx").astype(jnp.int32)[None]

    inputs = (queries, keys, values, grad_out)
    owned = exchange(own_states(*inputs), "ctx")
    *parts, local = near(inputs, node_ids, flags)
    states = exchange(scan(spot, owned, local), "ctx")

    terms = exchange(gathered(states, lax.axis_size("dp")), "dp")
    norm_tokens = lax.axis_size("dp") * length * lax.axis_size("ctx") * HD
    grad_gain = jnp.sum(terms, axis=0)[0, :H] * scale / math.sqrt(norm_tokens)

    return (*far(scale, gain, keys, values, grad_out, parts, states), grad_gain)


def solution(mesh):
    placed = (
        P("dp", "ctx", None),
        P("dp", "ctx", None),
        P("dp", "ctx", None),
        P("dp", "ctx", None),
        P("dp", "ctx"),
        P("dp", "ctx"),
        P(),
    )
    return jax.shard_map(
        on_device,
        mesh=mesh,
        in_specs=placed,
        out_specs=(P("dp", "ctx", None), P("dp", "ctx", None), P("dp", "ctx", None), P()),
        check_vma=False,
    )
```
